32 devices in a mesh: wide: 8 (over y, x, core), narrow: 4 (over z).
Axes of the slice: x: 2, y: 2, z: 4, core: 2. Of those that a mesh axis runs over, the one named last changes fastest.
Arguments:
- batch_index: int32 [256], P('narrow'), may hold values from 0 to 255
- train_features: float32 [1024, 1024], P('narrow'), may hold values from -6 to 6
- train_labels: float32 [1024, 1000], P('narrow'), may hold values from -12 to 12
- centers: float32 [8192, 1024], P(('wide', 'narrow')), may hold values from -6 to 6
- weights: float32 [8192, 1000], P(('wide', 'narrow')), may hold values from -6 to 6
Outputs:
- new_weights: float32 [8192, 1000], P(('wide', 'narrow'))
- residual: float32 [256, 1000], P('narrow')
The draws below stay inside these ranges and needn't reach their ends.
Inputs may be any that keep to these rules, and one draw needn't show every extreme that they name: `batch_index`: entry i names a row of the training shard held by narrow index i // 64.
All inputs are finite; a program needn't handle non-finite values.
Results may differ from the reference program's by a relative error of at most 0.0001.
Values sent between devices are 32-bit elements; how exact they have to be, the bound alone decides.
A program may use at most 64 MiB of HBM per device.

```python
import math
import jax
import jax.numpy as jnp
from jax import lax

D = 1024
L = 1000
M_DEV = 256
BLOCK = 64
TRAIN_DEV = 256
BATCH = 256
CENTERS = 8192
TRAIN = 1024
N_WIDE = 8
N_NARROW = 4


def shaped_rows(key, offset, row_count):
    own_key = jax.random.fold_in(key, offset)
    entry_key, norm_key = jax.random.split(own_key)
    sample = jax.random.normal(entry_key, (row_count, D), jnp.float32)
    square = jax.random.uniform(norm_key, (row_count, 1), jnp.float32, 0.85, 1.15)
    length = jnp.sqrt(jnp.sum(sample * sample, axis=1, keepdims=True))
    return jnp.clip(sample * jnp.sqrt(square * D) / length, -6.0, 6.0)


def draw_train_features(key, part):
    return shaped_rows(key, 11, TRAIN)


def draw_centers(key, part):
    return shaped_rows(key, 23, CENTERS)


def with_ends(values, rng, low, high):
    extent = values.shape
    index_at = [jax.random.randint(jax.random.fold_in(rng, axis), (), 0, extent[axis]) for axis in range(len(extent))]
    values = values.at[tuple(index_at)].set(low)
    longest = extent.index(max(extent))
    index_at[longest] = (index_at[longest] + 1) % extent[longest]
    return values.at[tuple(index_at)].set(high)


def shard_levels(rng, dims, shards, least, top_value):
    loudness = 1.0
    for position, blocks in shards:
        draws = jax.random.uniform(jax.random.fold_in(jax.random.fold_in(rng, 6), position), (blocks,), jnp.float32, least / len(shards), top_value / len(shards))
        loudness = loudness * jnp.repeat(jnp.exp(draws), dims[position] // blocks).reshape((-1,) + (1,) * (len(dims) - 1 - position))
    return loudness


def centred(key, dims, deviation, reach, shards=(), kind=jnp.bfloat16):
    drawn = jax.random.normal(key, dims, jnp.float32) * deviation
    if len(shards) > 0:
        drawn = shard_levels(key, dims, shards, -0.22, 0.18) * drawn
    return jnp.clip(drawn, min=-reach, max=reach).astype(kind)


def setup_inputs(seed: int = 0) -> dict:
    arg_keys = jax.random.split(jax.random.key(seed), 6)
    return {
        "batch_index": with_ends(jax.random.randint(arg_keys[0], (BATCH,), 0, TRAIN_DEV), jax.random.fold_in(arg_keys[0], 1), 0, TRAIN_DEV - 1).astype(jnp.int32),
        "train_features": draw_train_features(jax.random.fold_in(arg_keys[5], 71), 0),
        "train_labels": centred(arg_keys[2], (TRAIN, L), 2.0, 12.0, ((0, 4),), jnp.float32),
        "centers": draw_centers(jax.random.fold_in(arg_keys[5], 71), 0),
        "weights": centred(arg_keys[4], (CENTERS, L), 1.0, 6.0, ((0, 32),), jnp.float32),
    }


step_size = 1.0

def kernel_block(rows, centers_blk):
    inner = jnp.dot(rows, centers_blk.T, precision=lax.Precision.HIGHEST, preferred_element_type=jnp.float32)
    row_sq = lax.optimization_barrier(jnp.sum(rows * rows, axis=1))
    center_sq = lax.optimization_barrier(jnp.sum(centers_blk * centers_blk, axis=1))
    return jnp.exp((2.0 * rows.shape[1] - row_sq[:, None] - center_sq[None, :] + 2.0 * inner) / 128.0)

def reference(batch_index, train_features, train_labels, centers, weights):
    picks = jnp.arange(BATCH, dtype=jnp.int32) // BLOCK * TRAIN_DEV + batch_index.astype(jnp.int32)
    rows = jnp.take(train_features, picks, axis=0)
    targets = jnp.take(train_labels, picks, axis=0)
    groups = N_WIDE * N_NARROW
    center_blocks = centers.reshape(groups, M_DEV, D)
    weight_blocks = weights.reshape(groups, M_DEV, L)

    def accumulate(total, pair):
        kern = kernel_block(rows, pair[0])
        return (total + jnp.dot(kern, pair[1], precision=lax.Precision.HIGHEST, preferred_element_type=jnp.float32), None)
    partial_value, _ = lax.scan(accumulate, jnp.zeros((BATCH, L), jnp.float32), (center_blocks, weight_blocks))
    residual = partial_value * (1.0 / math.sqrt(CENTERS)) - targets

    def update(pair):
        kern = kernel_block(rows, pair[0])
        delta = lax.dot_general(kern, residual, (((0,), (0,)), ((), ())), precision=lax.Precision.HIGHEST, preferred_element_type=jnp.float32)
        return pair[1] - step_size / BATCH * delta
    new_weights = lax.map(update, (center_blocks, weight_blocks)).reshape(CENTERS, L)
    return (new_weights, residual)
```

```python
import functools
import math

import jax
import jax.numpy as jnp
from jax import lax
from jax.experimental import pallas as pl
from jax.experimental.pallas import tpu as pltpu
from jax.sharding import PartitionSpec as P

step_size = 1.0
MESH = pl.DeviceIdType.MESH
HIGHEST = lax.Precision.HIGHEST
SUB = 8


def dot(a, b, dims):
    return lax.dot_general(
        a, b, (dims, ((), ())), precision=HIGHEST, preferred_element_type=jnp.float32
    )


def plan(wide, block):
    stages, rows = [], block
    for _ in range(wide.bit_length() - 1):
        halves = rows >= 2 * SUB
        rows = rows // 2 if halves else rows
        stages.append((rows, halves))
    return stages


def step_kernel(
    wide, narrow, count, index_ref, tf_hbm, lab_hbm, cen_hbm, wgt_hbm, out_hbm, res_hbm,
    tf, lab, cen, wgt, rows, kern, part, resid, tgt, got, zgot, load_sem,
    zrow_s, zrow_r, crow_s, crow_r, red_s, red_r, zred_s, zred_r, zag_s, zag_r, ag_s, ag_r, out_sem,
):
    w, n = lax.axis_index("wide"), lax.axis_index("narrow")
    block = index_ref.shape[0]
    batch = block * narrow
    features = cen.shape[1]
    stages = plan(wide, block)
    nst = len(stages)
    core = w % 2
    partner = (w + 1 - 2 * core, n)
    up = [2**k for k in range(1, nst)]
    masks = [1] + [jnp.where(core == 0, p, q) for p, q in zip(up, up[::-1])]
    side = [core] + [(w // m) % 2 for m in masks[1:]]
    peer = [partner] + [(w + m * (1 - 2 * s), n) for m, s in zip(masks[1:], side[1:])]
    start = [0]
    for s, (held, halves) in zip(side, stages):
        start.append(start[-1] + (s * held if halves else 0))
    start = [0] + [pl.multiple_of(s, SUB) for s in start[1:]]
    half = stages[0][0]

    loads = [
        pltpu.make_async_copy(src, dst, load_sem.at[i])
        for i, (src, dst) in enumerate(((tf_hbm, tf), (cen_hbm, cen), (wgt_hbm, wgt), (lab_hbm, lab)))
    ]
    for load in loads:
        load.start()
    zpeers = [(w, lax.rem(n + k, narrow)) for k in range(1, narrow)]
    barrier = pltpu.get_barrier_semaphore()
    for p in zpeers + peer:
        pl.semaphore_signal(barrier, inc=1, device_id=p, device_id_type=MESH)

    def copy(src, dst, ssem, rsem, to):
        return pltpu.make_async_remote_copy(
            src_ref=src, dst_ref=dst, send_sem=ssem, recv_sem=rsem, device_id=to, device_id_type=MESH
        )

    sent = []

    def send(*args, later=True):
        c = copy(*args)
        c.start()
        if later:
            sent.append(c)
        return c

    loads[0].wait()
    for g in range(block // SUB):
        picked = [tf[pl.ds(index_ref[g * SUB + i], 1), :] for i in range(SUB)]
        rows[n, pl.ds(g * SUB, SUB), :] = jnp.concatenate(picked, axis=0)
    pl.semaphore_wait(barrier, len(zpeers) + nst)

    mine = pl.ds(start[1], half)
    other = pl.ds(pl.multiple_of((1 - core) * half, SUB), half)
    for k in range(1, narrow):
        to = (w, lax.rem(n + narrow - k, narrow))
        send(rows.at[n, mine], rows.at[n, mine], zrow_s.at[k], zrow_r.at[k], to)

    loads[1].wait()
    centers = cen[...]
    ones = jnp.ones((SUB, features), jnp.float32)
    center_sq = dot(ones, centers * centers, ((1,), (1,)))[0:1, :]

    def at(k):
        return lax.rem(n + k, narrow)

    def forward(k):
        m = at(k)
        copy(rows.at[m, mine], rows.at[m, mine], zrow_s.at[k], zrow_r.at[k], partner).wait_recv()
        send(rows.at[m, mine], rows.at[m, mine], crow_s.at[k], crow_r.at[k], partner)

    def reduce_copy(j, k):
        m = at(k)
        held, halves = stages[j]
        first = pl.multiple_of(start[j] + (1 - side[j]) * held, SUB) if halves else start[j + 1]
        return (
            part.at[m, pl.ds(first, held)], got[j].at[k], red_s.at[j, k], red_r.at[j, k], peer[j]
        )

    sends = {}

    def begin(k):
        m = at(k)
        if k > 0:
            copy(rows.at[m, other], rows.at[m, other], crow_s.at[k], crow_r.at[k], partner).wait_recv()
        piece = rows[m]
        inner = dot(piece, cen[...], ((1,), (1,)))
        piece_sq = jnp.sum(piece * piece, axis=1, keepdims=True)
        value = jnp.exp((2.0 * features - piece_sq - center_sq + 2.0 * inner) / 128.0)
        kern[m] = value
        if k == 0:
            loads[2].wait()
        part[m] = dot(value, wgt[...], ((1,), (1,)))
        sends[0, k] = send(*reduce_copy(0, k), later=stages[0][1])

    def reduce(j, k):
        m = at(k)
        held, halves = stages[j]
        copy(*reduce_copy(j, k)).wait_recv()
        if not halves:
            sends[j, k].wait_send()
        keep = pl.ds(start[j + 1], held)
        part[m, keep, :] = part[m, keep, :] + got[j][k]
        if j + 1 < nst:
            sends[j + 1, k] = send(*reduce_copy(j + 1, k), later=stages[j + 1][1])
        elif k > 0:
            send(part.at[m, keep], zgot.at[k], zred_s.at[k], zred_r.at[k], (w, m))

    for t in range(narrow + nst):
        if t < narrow:
            begin(t)
        if t + 1 < narrow:
            forward(t + 1)
        for j in range(nst):
            if 0 <= t - 1 - j < narrow:
                reduce(j, t - 1 - j)

    last = stages[-1][0]
    keep = pl.ds(start[nst], last)
    loads[3].wait()
    column = lax.broadcasted_iota(jnp.int32, (1, lab.shape[1]), 1)
    chosen = [jnp.where(column == index_ref[start[nst] + i], 1.0, 0.0) for i in range(last)]
    tgt[...] = dot(jnp.concatenate(chosen, axis=0), lab[...], ((1,), (1,)))
    total = part[n, keep, :]
    for k in range(1, narrow):
        copy(part.at[n, keep], zgot.at[k], zred_s.at[k], zred_r.at[k], partner).wait_recv()
        total = total + zgot[k]
    resid[n, keep, :] = total * (1.0 / math.sqrt(count)) - tgt[...]

    for k in range(1, narrow):
        to = (w, lax.rem(n + narrow - k, narrow))
        send(resid.at[n, keep], resid.at[n, keep], zag_s.at[k], zag_r.at[k], to)

    back = [j for j in range(nst) if stages[j][1]][::-1]

    def spread(i, k):
        m = at(k)
        if i == 0:
            if k > 0:
                copy(resid.at[m, keep], resid.at[m, keep], zag_s.at[k], zag_r.at[k], partner).wait_recv()
        else:
            j = back[i - 1]
            held = stages[j][0]
            sibling = pl.ds(pl.multiple_of(start[j] + (1 - side[j]) * held, SUB), held)
            copy(
                resid.at[m, sibling], resid.at[m, sibling], ag_s.at[j, k], ag_r.at[j, k], peer[j]
            ).wait_recv()
        if i < len(back):
            j = back[i]
            own = pl.ds(start[j + 1], stages[j][0])
            send(resid.at[m, own], resid.at[m, own], ag_s.at[j, k], ag_r.at[j, k], peer[j])

    res_copy = pltpu.make_async_copy(resid.at[n], res_hbm, out_sem.at[0])
    for t in range(narrow + len(back)):
        for i in range(len(back) + 1):
            if 0 <= t - i < narrow:
                spread(i, t - i)
                if i == len(back) and t - i == 0:
                    res_copy.start()

    every = resid[...].reshape(batch, resid.shape[2])
    delta = dot(every, kern[...].reshape(batch, cen.shape[0]), ((0,), (0,)))
    wgt[...] = wgt[...] - step_size / batch * delta
    out_copy = pltpu.make_async_copy(wgt, out_hbm, out_sem.at[1])
    out_copy.start()
    for c in sent:
        c.wait_send()
    res_copy.wait()
    out_copy.wait()


def per_device(batch_index, train_features, train_labels, centers, weights):
    wide, narrow = lax.axis_size("wide"), lax.axis_size("narrow")
    block, features = batch_index.shape[0], centers.shape[1]
    outputs, owned = weights.shape[1], centers.shape[0]
    labels_t, weights_t = train_labels.T, weights.T
    stages = plan(wide, block)
    nst, last = len(stages), stages[-1][0]
    f32, dma = jnp.float32, pltpu.SemaphoreType.DMA
    anywhere = pl.BlockSpec(memory_space=pl.ANY)
    new_weights_t, residual = pl.pallas_call(
        functools.partial(step_kernel, wide, narrow, owned * wide * narrow),
        out_shape=(
            jax.ShapeDtypeStruct(weights_t.shape, f32),
            jax.ShapeDtypeStruct((block, outputs), f32),
        ),
        in_specs=[pl.BlockSpec(memory_space=pltpu.SMEM)] + [anywhere] * 4,
        out_specs=(anywhere, anywhere),
        scratch_shapes=[
            pltpu.VMEM(train_features.shape, f32),
            pltpu.VMEM(labels_t.shape, f32),
            pltpu.VMEM(centers.shape, f32),
            pltpu.VMEM(weights_t.shape, f32),
            pltpu.VMEM((narrow, block, features), f32),
            pltpu.VMEM((narrow, block, owned), f32),
            pltpu.VMEM((narrow, block, outputs), f32),
            pltpu.VMEM((narrow, block, outputs), f32),
            pltpu.VMEM((last, outputs), f32),
            [pltpu.VMEM((narrow, held, outputs), f32) for held, _ in stages],
            pltpu.VMEM((narrow, last, outputs), f32),
            dma((4,)),
            dma((narrow,)), dma((narrow,)),
            dma((narrow,)), dma((narrow,)),
            dma((nst, narrow)), dma((nst, narrow)),
            dma((narrow,)), dma((narrow,)),
            dma((narrow,)), dma((narrow,)),
            dma((nst, narrow)), dma((nst, narrow)),
            dma((2,)),
        ],
        compiler_params=pltpu.CompilerParams(
            collective_id=0, has_side_effects=True, vmem_limit_bytes=60 * 2**20
        ),
    )(batch_index, train_features, labels_t, centers, weights_t)
    return new_weights_t.T, residual


def solution(mesh):
    in_specs = (
        P("narrow"),
        P("narrow", None),
        P("narrow", None),
        P(("wide", "narrow"), None),
        P(("wide", "narrow"), None),
    )
    out_specs = (P(("wide", "narrow"), None), P("narrow", None))
    return jax.shard_map(
        per_device, mesh=mesh, in_specs=in_specs, out_specs=out_specs, check_vma=False
    )
```

```python
import functools
import math

import jax
import jax.numpy as jnp
from jax import lax
from jax.experimental import pallas as pl
from jax.experimental.pallas import tpu as pltpu
from jax.sharding import PartitionSpec as P

step_size = 1.0
MESH = pl.DeviceIdType.MESH
HIGHEST = lax.Precision.HIGHEST
ROW_DEPTH = 3
SUB = 8


def dot(a, b, dims):
    return lax.dot_general(
        a, b, (dims, ((), ())), precision=HIGHEST, preferred_element_type=jnp.float32
    )


def plan(wide, block):
    stages, rows = [], block
    for _ in range(wide.bit_length() - 1):
        halves = rows >= 2 * SUB
        rows = rows // 2 if halves else rows
        stages.append((rows, halves))
    return stages


def step_kernel(
    wide, narrow, count, index_ref, tf_hbm, lab_hbm, cen_hbm, wgt_hbm, out_hbm, res_hbm,
    tf, lab, cen, wgt, rows, kern, away, part, resid, tgt, got, zgot, load_sem,
    zrow_s, zrow_r, row_s, row_r, pair_s, pair_r, kern_s, kern_r, red_s, red_r, zred_s, zred_r, zag_s, zag_r, ag_s, ag_r, out_sem,
):
    w, n = lax.axis_index("wide"), lax.axis_index("narrow")
    block = index_ref.shape[0]
    batch = block * narrow
    features, owned = cen.shape[2], cen.shape[1]
    stages = plan(wide, block)
    nst = len(stages)
    core = w % 2
    partner = (w + 1 - 2 * core, n)
    up = [2**k for k in range(1, nst)]
    masks = [1] + [jnp.where(core == 0, p, q) for p, q in zip(up, up[::-1])]
    side = [core] + [(w // m) % 2 for m in masks[1:]]
    peer = [partner] + [(w + m * (1 - 2 * s), n) for m, s in zip(masks[1:], side[1:])]
    start = [0]
    for s, (held, halves) in zip(side, stages):
        start.append(start[-1] + (s * held if halves else 0))
    start = [0] + [pl.multiple_of(s, SUB) for s in start[1:]]
    half = stages[0][0]

    loads = [
        pltpu.make_async_copy(src, dst, load_sem.at[i])
        for i, (src, dst) in enumerate(((tf_hbm, tf), (cen_hbm, cen.at[0]), (wgt_hbm, wgt.at[0]), (lab_hbm, lab)))
    ]
    for load in loads:
        load.start()
    zpeers = [(w, lax.rem(n + k, narrow)) for k in range(1, narrow)]
    barrier = pltpu.get_barrier_semaphore()
    for p in zpeers + peer:
        pl.semaphore_signal(barrier, inc=1, device_id=p, device_id_type=MESH)

    def copy(src, dst, ssem, rsem, to):
        return pltpu.make_async_remote_copy(
            src_ref=src, dst_ref=dst, send_sem=ssem, recv_sem=rsem, device_id=to, device_id_type=MESH
        )

    sent = []

    def send(*args, later=True):
        c = copy(*args)
        c.start()
        if later:
            sent.append(c)
        return c

    loads[0].wait()
    for g in range(block // SUB):
        picked = [tf[pl.ds(index_ref[g * SUB + i], 1), :] for i in range(SUB)]
        rows[n, pl.ds(g * SUB, SUB), :] = jnp.concatenate(picked, axis=0)
    pl.semaphore_wait(barrier, len(zpeers) + nst)

    def at(k):
        return lax.rem(n + k, narrow)

    def piece_of(j):
        held = stages[j][0]
        theirs = pl.multiple_of(start[j] + (1 - side[j]) * held, SUB)
        return pl.ds(start[j + 1], held), pl.ds(theirs, held)

    def spread(ref, zsem, sem, back, i, k):
        m = at(k)
        if i == 0:
            if k > 0:
                held = piece_of(back[0])[0]
                copy(ref.at[m, held], ref.at[m, held], zsem[0].at[k], zsem[1].at[k], partner).wait_recv()
        else:
            j = back[i - 1]
            theirs = piece_of(j)[1]
            copy(ref.at[m, theirs], ref.at[m, theirs], sem[0].at[j, k], sem[1].at[j, k], peer[j]).wait_recv()
        if i < len(back) and not (i == len(back) - 1 and back[i] == 0 and ref is rows):
            j = back[i]
            held = piece_of(j)[0]
            send(ref.at[m, held], ref.at[m, held], sem[0].at[j, k], sem[1].at[j, k], peer[j])

    def along_narrow(ref, held, zsem):
        for k in range(1, narrow):
            to = (w, lax.rem(n + narrow - k, narrow))
            send(ref.at[n, held], ref.at[n, held], zsem[0].at[k], zsem[1].at[k], to)

    cuts = [j for j in range(nst) if stages[j][1]][::-1]
    row_cuts = [j for j in cuts if j < ROW_DEPTH]
    mine, other = piece_of(0)
    along_narrow(rows, piece_of(row_cuts[0])[0], (zrow_s, zrow_r))

    loads[1].wait()
    send(cen.at[0], cen.at[1], pair_s.at[0], pair_r.at[0], partner)
    loads[2].wait()
    send(wgt.at[0], wgt.at[1], pair_s.at[1], pair_r.at[1], partner)
    ones = jnp.ones((SUB, features), jnp.float32)

    def squares(o):
        centers = cen[o]
        return dot(ones, centers * centers, ((1,), (1,)))[0:1, :]

    center_sq = [squares(0)]

    def reduce_copy(j, k):
        m = at(k)
        held, halves = stages[j]
        first = start[j] + (1 - side[j]) * held if halves else start[j + 1]
        first = pl.multiple_of(first - core * half, SUB)
        return (
            part.at[m, pl.ds(first, held)], got[j - 1].at[k], red_s.at[j, k], red_r.at[j, k], peer[j]
        )

    sends = {}

    def begin(ks):
        piece = jnp.concatenate([rows[at(k), mine, :] for k in ks], axis=0)
        piece_sq = jnp.sum(piece * piece, axis=1, keepdims=True)
        total = 0.0
        for o in range(2):
            if len(center_sq) == o:
                copy(cen.at[0], cen.at[1], pair_s.at[0], pair_r.at[0], partner).wait_recv()
                center_sq.append(squares(o))
            inner = dot(piece, cen[o], ((1,), (1,)))
            value = jnp.exp((2.0 * features - piece_sq - center_sq[o] + 2.0 * inner) / 128.0)
            for i, k in enumerate(ks):
                this = value[i * half : (i + 1) * half, :]
                if o == 0:
                    kern[at(k), mine, :] = this
                else:
                    away[k] = this
            if o == 1 and 0 in ks:
                copy(wgt.at[0], wgt.at[1], pair_s.at[1], pair_r.at[1], partner).wait_recv()
            total = total + dot(value, wgt[o], ((1,), (1,)))
        for i, k in enumerate(ks):
            part[at(k)] = total[i * half : (i + 1) * half, :]
        for k in ks:
            sends[1, k] = send(*reduce_copy(1, k), later=stages[1][1])
        for k in ks:
            send(away.at[k], kern.at[at(k), mine], kern_s.at[k], kern_r.at[k], partner)

    def reduce(j, k):
        m = at(k)
        held, halves = stages[j]
        copy(*reduce_copy(j, k)).wait_recv()
        if not halves:
            sends[j, k].wait_send()
        keep = pl.ds(pl.multiple_of(start[j + 1] - core * half, SUB), held)
        part[m, keep, :] = part[m, keep, :] + got[j - 1][k]
        if j + 1 < nst:
            sends[j + 1, k] = send(*reduce_copy(j + 1, k), later=stages[j + 1][1])
        elif k > 0:
            send(part.at[m, keep], zgot.at[k], zred_s.at[k], zred_r.at[k], (w, m))

    begin([0])
    for i in range(len(row_cuts)):
        for k in range(1, narrow):
            spread(rows, (zrow_s, zrow_r), (row_s, row_r), row_cuts, i, k)
        if i + 1 < nst:
            reduce(i + 1, 0)
    for i in range(len(row_cuts) + 1, nst):
        reduce(i, 0)
    begin(list(range(1, narrow)))
    for j in range(1, nst):
        for k in range(1, narrow):
            reduce(j, k)

    last = stages[-1][0]
    keep = pl.ds(start[nst], last)
    loads[3].wait()
    column = lax.broadcasted_iota(jnp.int32, (1, lab.shape[1]), 1)
    chosen = [jnp.where(column == index_ref[start[nst] + i], 1.0, 0.0) for i in range(last)]
    tgt[...] = dot(jnp.concatenate(chosen, axis=0), lab[...], ((1,), (1,)))
    own = pl.ds(pl.multiple_of(start[nst] - core * half, SUB), last)
    total = part[n, own, :]
    for k in range(1, narrow):
        copy(part.at[n, own], zgot.at[k], zred_s.at[k], zred_r.at[k], partner).wait_recv()
        total = total + zgot[k]
    resid[n, keep, :] = total * (1.0 / math.sqrt(count)) - tgt[...]

    along_narrow(resid, keep, (zag_s, zag_r))
    res_copy = pltpu.make_async_copy(resid.at[n], res_hbm, out_sem.at[0])
    for t in range(narrow + len(cuts)):
        for i in range(len(cuts) + 1):
            if 0 <= t - i < narrow:
                spread(resid, (zag_s, zag_r), (ag_s, ag_r), cuts, i, t - i)
                if i == len(cuts) and t - i == 0:
                    res_copy.start()

    for k in range(narrow):
        copy(away.at[k], kern.at[at(k), other], kern_s.at[k], kern_r.at[k], partner).wait_recv()
    for c in sent:
        c.wait_send()
    every = resid[...].reshape(batch, resid.shape[2])
    delta = dot(every, kern[...].reshape(batch, owned), ((0,), (0,)))
    wgt[0] = wgt[0] - step_size / batch * delta
    out_copy = pltpu.make_async_copy(wgt.at[0], out_hbm, out_sem.at[1])
    out_copy.start()
    res_copy.wait()
    out_copy.wait()


def per_device(batch_index, train_features, train_labels, centers, weights):
    wide, narrow = lax.axis_size("wide"), lax.axis_size("narrow")
    block, features = batch_index.shape[0], centers.shape[1]
    outputs, owned = weights.shape[1], centers.shape[0]
    labels_t, weights_t = train_labels.T, weights.T
    stages = plan(wide, block)
    nst, last = len(stages), stages[-1][0]
    f32, dma = jnp.float32, pltpu.SemaphoreType.DMA
    anywhere = pl.BlockSpec(memory_space=pl.ANY)
    new_weights_t, residual = pl.pallas_call(
        functools.partial(step_kernel, wide, narrow, owned * wide * narrow),
        out_shape=(
            jax.ShapeDtypeStruct(weights_t.shape, f32),
            jax.ShapeDtypeStruct((block, outputs), f32),
        ),
        in_specs=[pl.BlockSpec(memory_space=pltpu.SMEM)] + [anywhere] * 4,
        out_specs=(anywhere, anywhere),
        scratch_shapes=[
            pltpu.VMEM(train_features.shape, f32),
            pltpu.VMEM(labels_t.shape, f32),
            pltpu.VMEM((2, *centers.shape), f32),
            pltpu.VMEM((2, *weights_t.shape), f32),
            pltpu.VMEM((narrow, block, features), f32),
            pltpu.VMEM((narrow, block, owned), f32),
            pltpu.VMEM((narrow, block // 2, owned), f32),
            pltpu.VMEM((narrow, block // 2, outputs), f32),
            pltpu.VMEM((narrow, block, outputs), f32),
            pltpu.VMEM((last, outputs), f32),
            [pltpu.VMEM((narrow, held, outputs), f32) for held, _ in stages[1:]],
            pltpu.VMEM((narrow, last, outputs), f32),
            dma((4,)),
            dma((narrow,)), dma((narrow,)),
            dma((nst, narrow)), dma((nst, narrow)),
            dma((2,)), dma((2,)),
            dma((narrow,)), dma((narrow,)),
            dma((nst, narrow)), dma((nst, narrow)),
            dma((narrow,)), dma((narrow,)),
            dma((narrow,)), dma((narrow,)),
            dma((nst, narrow)), dma((nst, narrow)),
            dma((2,)),
        ],
        compiler_params=pltpu.CompilerParams(
            collective_id=0, has_side_effects=True, vmem_limit_bytes=60 * 2**20
        ),
    )(batch_index, train_features, labels_t, centers, weights_t)
    return new_weights_t.T, residual


def solution(mesh):
    in_specs = (
        P("narrow"),
        P("narrow", None),
        P("narrow", None),
        P(("wide", "narrow"), None),
        P(("wide", "narrow"), None),
    )
    out_specs = (P(("wide", "narrow"), None), P("narrow", None))
    return jax.shard_map(
        per_device, mesh=mesh, in_specs=in_specs, out_specs=out_specs, check_vma=False
    )
```

```python
import functools
import math

import jax
import jax.numpy as jnp
from jax import lax
from jax.experimental import pallas as pl
from jax.experimental.pallas import tpu as pltpu
from jax.sharding import PartitionSpec as P

step_size = 1.0
MESH = pl.DeviceIdType.MESH
HIGHEST = lax.Precision.HIGHEST
ROW_DEPTH = 2
SUB = 8


def dot(a, b, dims):
    return lax.dot_general(
        a, b, (dims, ((), ())), precision=HIGHEST, preferred_element_type=jnp.float32
    )


def split(x, count):
    terms = []
    for _ in range(count):
        terms.append(x.astype(jnp.bfloat16))
        x = x - terms[-1].astype(jnp.float32)
    return terms


def split_dot(a, b):
    held = a[0].shape[0]
    orders = [[] for _ in a]
    for i, right in enumerate(b):
        left = a[: len(a) - i]
        out = lax.dot_general(
            jnp.concatenate(left, axis=0), right, (((1,), (1,)), ((), ())),
            preferred_element_type=jnp.float32,
        )
        for j in range(len(left)):
            orders[i + j].append(out[j * held : (j + 1) * held])
    total = 0.0
    for terms in orders[::-1]:
        total = total + sum(terms)
    return total


def plan(wide, block):
    stages, rows = [], block
    for _ in range(wide.bit_length() - 1):
        halves = rows >= 2 * SUB
        rows = rows // 2 if halves else rows
        stages.append((rows, halves))
    return stages


def step_kernel(
    wide, narrow, count, index_ref, tf_hbm, lab_hbm, cen_hbm, wgt_hbm, kern_hbm, all_hbm, res_hbm,
    tf, lab, cen, wgt, cen_terms, wgt_terms, rows, kern, away, part, resid, tgt, got, zgot, load_sem,
    zrow_s, zrow_r, row_s, row_r, pair_s, pair_r, kern_s, kern_r, red_s, red_r, zred_s, zred_r, zag_s, zag_r, ag_s, ag_r, out_sem,
):
    w, n = lax.axis_index("wide"), lax.axis_index("narrow")
    block = index_ref.shape[0]
    batch = block * narrow
    features, owned = cen.shape[2], cen.shape[1]
    stages = plan(wide, block)
    nst = len(stages)
    core = w % 2
    partner = (w + 1 - 2 * core, n)
    up = [2**k for k in range(1, nst)]
    masks = [1] + [jnp.where(core == 0, p, q) for p, q in zip(up, up[::-1])]
    side = [core] + [(w // m) % 2 for m in masks[1:]]
    peer = [partner] + [(w + m * (1 - 2 * s), n) for m, s in zip(masks[1:], side[1:])]
    start = [0]
    for s, (held, halves) in zip(side, stages):
        start.append(start[-1] + (s * held if halves else 0))
    start = [0] + [pl.multiple_of(s, SUB) for s in start[1:]]
    half = stages[0][0]

    loads = [
        pltpu.make_async_copy(src, dst, load_sem.at[i])
        for i, (src, dst) in enumerate(((tf_hbm, tf), (cen_hbm, cen.at[0]), (wgt_hbm, wgt.at[0]), (lab_hbm, lab)))
    ]
    for load in loads:
        load.start()
    zpeers = [(w, lax.rem(n + k, narrow)) for k in range(1, narrow)]
    barrier = pltpu.get_barrier_semaphore()
    for p in zpeers + peer:
        pl.semaphore_signal(barrier, inc=1, device_id=p, device_id_type=MESH)

    def copy(src, dst, ssem, rsem, to):
        return pltpu.make_async_remote_copy(
            src_ref=src, dst_ref=dst, send_sem=ssem, recv_sem=rsem, device_id=to, device_id_type=MESH
        )

    sent = []

    def send(*args, later=True):
        c = copy(*args)
        c.start()
        if later:
            sent.append(c)
        return c

    loads[0].wait()
    for g in range(block // SUB):
        picked = [tf[pl.ds(index_ref[g * SUB + i], 1), :] for i in range(SUB)]
        rows[n, pl.ds(g * SUB, SUB), :] = jnp.concatenate(picked, axis=0)
    pl.semaphore_wait(barrier, len(zpeers) + nst)

    def at(k):
        return lax.rem(n + k, narrow)

    def piece_of(j):
        held = stages[j][0]
        theirs = pl.multiple_of(start[j] + (1 - side[j]) * held, SUB)
        return pl.ds(start[j + 1], held), pl.ds(theirs, held)

    def spread(ref, zsem, sem, back, i, k):
        m = at(k)
        if i == 0:
            if k > 0:
                held = piece_of(back[0])[0]
                copy(ref.at[m, held], ref.at[m, held], zsem[0].at[k], zsem[1].at[k], partner).wait_recv()
        else:
            j = back[i - 1]
            theirs = piece_of(j)[1]
            copy(ref.at[m, theirs], ref.at[m, theirs], sem[0].at[j, k], sem[1].at[j, k], peer[j]).wait_recv()
        if i < len(back) and not (i == len(back) - 1 and back[i] == 0 and ref is rows):
            j = back[i]
            held = piece_of(j)[0]
            send(ref.at[m, held], ref.at[m, held], sem[0].at[j, k], sem[1].at[j, k], peer[j])

    def along_narrow(ref, held, zsem):
        for k in range(1, narrow):
            to = (w, lax.rem(n + narrow - k, narrow))
            send(ref.at[n, held], ref.at[n, held], zsem[0].at[k], zsem[1].at[k], to)

    cuts = [j for j in range(nst) if stages[j][1]][::-1]
    row_cuts = [j for j in cuts if j < ROW_DEPTH]
    mine, other = piece_of(0)
    along_narrow(rows, piece_of(row_cuts[0])[0], (zrow_s, zrow_r))

    loads[1].wait()
    send(cen.at[0], cen.at[1], pair_s.at[0], pair_r.at[0], partner)
    loads[2].wait()
    send(wgt.at[0], wgt.at[1], pair_s.at[1], pair_r.at[1], partner)
    ones = jnp.ones((SUB, features), jnp.float32)

    def squares(o):
        centers = cen[o]
        for i, term in enumerate(split(centers, 3)):
            cen_terms[o, i] = term
        return dot(ones, centers * centers, ((1,), (1,)))[0:1, :]

    center_sq = [squares(0)]

    def reduce_copy(j, k):
        m = at(k)
        held, halves = stages[j]
        first = start[j] + (1 - side[j]) * held if halves else start[j + 1]
        first = pl.multiple_of(first - core * half, SUB)
        return (
            part.at[m, pl.ds(first, held)], got[j - 1].at[k], red_s.at[j, k], red_r.at[j, k], peer[j]
        )

    sends = {}

    def begin(ks):
        piece = jnp.concatenate([rows[at(k), mine, :] for k in ks], axis=0)
        piece_sq = jnp.sum(piece * piece, axis=1, keepdims=True)
        piece_terms = split(piece, 3)
        total = 0.0
        for o in range(2):
            if len(center_sq) == o:
                copy(cen.at[0], cen.at[1], pair_s.at[0], pair_r.at[0], partner).wait_recv()
                center_sq.append(squares(o))
            inner = split_dot(piece_terms, [cen_terms[o, i] for i in range(3)])
            value = jnp.exp((2.0 * features - piece_sq - center_sq[o] + 2.0 * inner) / 128.0)
            for i, k in enumerate(ks):
                this = value[i * half : (i + 1) * half, :]
                if o == 0:
                    kern[at(k), mine, :] = this
                else:
                    away[k] = this
            if o == 1 and 0 in ks:
                copy(wgt.at[0], wgt.at[1], pair_s.at[1], pair_r.at[1], partner).wait_recv()
            if 0 in ks:
                for i, term in enumerate(split(wgt[o], 2)):
                    wgt_terms[o, i] = term
            total = total + split_dot(split(value, 2), [wgt_terms[o, i] for i in range(2)])
        for i, k in enumerate(ks):
            part[at(k)] = total[i * half : (i + 1) * half, :]
        for k in ks:
            sends[1, k] = send(*reduce_copy(1, k), later=stages[1][1])
        for k in ks:
            send(away.at[k], kern.at[at(k), mine], kern_s.at[k], kern_r.at[k], partner)

    def reduce(j, k):
        m = at(k)
        held, halves = stages[j]
        copy(*reduce_copy(j, k)).wait_recv()
        if not halves:
            sends[j, k].wait_send()
        keep = pl.ds(pl.multiple_of(start[j + 1] - core * half, SUB), held)
        part[m, keep, :] = part[m, keep, :] + got[j - 1][k]
        if j + 1 < nst:
            sends[j + 1, k] = send(*reduce_copy(j + 1, k), later=stages[j + 1][1])
        elif k > 0:
            send(part.at[m, keep], zgot.at[k], zred_s.at[k], zred_r.at[k], (w, m))

    begin([0])
    for i in range(len(row_cuts)):
        for k in range(1, narrow):
            spread(rows, (zrow_s, zrow_r), (row_s, row_r), row_cuts, i, k)
        if i + 1 < nst:
            reduce(i + 1, 0)
    for i in range(len(row_cuts) + 1, nst):
        reduce(i, 0)
    begin(list(range(1, narrow)))
    for j in range(1, nst):
        for k in range(1, narrow):
            reduce(j, k)

    last = stages[-1][0]
    keep = pl.ds(start[nst], last)
    loads[3].wait()
    column = lax.broadcasted_iota(jnp.int32, (1, lab.shape[1]), 1)
    chosen = [jnp.where(column == index_ref[start[nst] + i], 1.0, 0.0) for i in range(last)]
    tgt[...] = dot(jnp.concatenate(chosen, axis=0), lab[...], ((1,), (1,)))
    own = pl.ds(pl.multiple_of(start[nst] - core * half, SUB), last)
    total = part[n, own, :]
    for k in range(1, narrow):
        copy(part.at[n, own], zgot.at[k], zred_s.at[k], zred_r.at[k], partner).wait_recv()
        total = total + zgot[k]
    resid[n, keep, :] = total * (1.0 / math.sqrt(count)) - tgt[...]

    along_narrow(resid, keep, (zag_s, zag_r))
    for k in range(narrow):
        copy(away.at[k], kern.at[at(k), other], kern_s.at[k], kern_r.at[k], partner).wait_recv()
    outs = [pltpu.make_async_copy(kern, kern_hbm, out_sem.at[0])]
    outs[0].start()
    for t in range(narrow + len(cuts)):
        for i in range(len(cuts) + 1):
            if 0 <= t - i < narrow:
                spread(resid, (zag_s, zag_r), (ag_s, ag_r), cuts, i, t - i)
                if i == len(cuts):
                    m = at(t - i)
                    outs.append(pltpu.make_async_copy(resid.at[m], all_hbm.at[m], out_sem.at[1 + t - i]))
                    outs[-1].start()
                    if t == i:
                        outs.append(pltpu.make_async_copy(resid.at[n], res_hbm, out_sem.at[1 + narrow]))
                        outs[-1].start()
    for c in sent:
        c.wait_send()
    for c in outs:
        c.wait()


def per_device(batch_index, train_features, train_labels, centers, weights):
    wide, narrow = lax.axis_size("wide"), lax.axis_size("narrow")
    block, features = batch_index.shape[0], centers.shape[1]
    outputs, owned = weights.shape[1], centers.shape[0]
    labels_t, weights_t = train_labels.T, weights.T
    stages = plan(wide, block)
    nst, last = len(stages), stages[-1][0]
    f32, dma = jnp.float32, pltpu.SemaphoreType.DMA
    anywhere = pl.BlockSpec(memory_space=pl.ANY)
    kernel, every, residual = pl.pallas_call(
        functools.partial(step_kernel, wide, narrow, owned * wide * narrow),
        out_shape=(
            jax.ShapeDtypeStruct((narrow, block, owned), f32),
            jax.ShapeDtypeStruct((narrow, block, outputs), f32),
            jax.ShapeDtypeStruct((block, outputs), f32),
        ),
        in_specs=[pl.BlockSpec(memory_space=pltpu.SMEM)] + [anywhere] * 4,
        out_specs=(anywhere, anywhere, anywhere),
        scratch_shapes=[
            pltpu.VMEM(train_features.shape, f32),
            pltpu.VMEM(labels_t.shape, f32),
            pltpu.VMEM((2, *centers.shape), f32),
            pltpu.VMEM((2, *weights_t.shape), f32),
            pltpu.VMEM((2, 3, *centers.shape), jnp.bfloat16),
            pltpu.VMEM((2, 2, *weights_t.shape), jnp.bfloat16),
            pltpu.VMEM((narrow, block, features), f32),
            pltpu.VMEM((narrow, block, owned), f32),
            pltpu.VMEM((narrow, block // 2, owned), f32),
            pltpu.VMEM((narrow, block // 2, outputs), f32),
            pltpu.VMEM((narrow, block, outputs), f32),
            pltpu.VMEM((last, outputs), f32),
            [pltpu.VMEM((narrow, held, outputs), f32) for held, _ in stages[1:]],
            pltpu.VMEM((narrow, last, outputs), f32),
            dma((4,)),
            dma((narrow,)), dma((narrow,)),
            dma((nst, narrow)), dma((nst, narrow)),
            dma((2,)), dma((2,)),
            dma((narrow,)), dma((narrow,)),
            dma((nst, narrow)), dma((nst, narrow)),
            dma((narrow,)), dma((narrow,)),
            dma((narrow,)), dma((narrow,)),
            dma((nst, narrow)), dma((nst, narrow)),
            dma((2 + narrow,)),
        ],
        compiler_params=pltpu.CompilerParams(
            collective_id=0, has_side_effects=True, vmem_limit_bytes=60 * 2**20
        ),
    )(batch_index, train_features, labels_t, centers, weights_t)
    batch = narrow * block
    delta = lax.dot_general(
        kernel.reshape(batch, owned), every.reshape(batch, outputs), (((0,), (0,)), ((), ())),
        precision=lax.Precision.HIGH, preferred_element_type=f32,
    )
    return weights - step_size / batch * delta, residual


def solution(mesh):
    in_specs = (
        P("narrow"),
        P("narrow", None),
        P("narrow", None),
        P(("wide", "narrow"), None),
        P(("wide", "narrow"), None),
    )
    out_specs = (P(("wide", "narrow"), None), P("narrow", None))
    return jax.shard_map(
        per_device, mesh=mesh, in_specs=in_specs, out_specs=out_specs, check_vma=False
    )
```

```python
import functools
import math

import jax
import jax.numpy as jnp
from jax import lax
from jax.experimental import pallas as pl
from jax.experimental.pallas import tpu as pltpu
from jax.sharding import PartitionSpec as P

step_size = 1.0
MESH = pl.DeviceIdType.MESH
HIGHEST = lax.Precision.HIGHEST
ROW_DEPTH = 2
SUB = 8


def dot(a, b, dims):
    return lax.dot_general(
        a, b, (dims, ((), ())), precision=HIGHEST, preferred_element_type=jnp.float32
    )


def split(x, count):
    terms = []
    for _ in range(count):
        terms.append(x.astype(jnp.bfloat16))
        x = x - terms[-1].astype(jnp.float32)
    return terms


def split_dot(a, b):
    held = a[0].shape[0]
    orders = [[] for _ in a]
    for i, right in enumerate(b):
        left = a[: len(a) - i]
        out = lax.dot_general(
            jnp.concatenate(left, axis=0), right, (((1,), (1,)), ((), ())),
            preferred_element_type=jnp.float32,
        )
        for j in range(len(left)):
            orders[i + j].append(out[j * held : (j + 1) * held])
    total = 0.0
    for terms in orders[::-1]:
        total = total + sum(terms)
    return total


def plan(wide, block):
    stages, rows = [], block
    for _ in range(wide.bit_length() - 1):
        halves = rows >= 2 * SUB
        rows = rows // 2 if halves else rows
        stages.append((rows, halves))
    return stages


def step_kernel(
    wide, narrow, count, index_ref, tf_hbm, lab_hbm, cen_hbm, wgt_hbm, kern_hbm, all_hbm, res_hbm,
    tf, lab, cen, wgt, cen_terms, wgt_terms, rows, kern, away, part, resid, tgt, got, zgot, load_sem,
    zrow_s, zrow_r, row_s, row_r, pair_s, pair_r, kern_s, kern_r, red_s, red_r, zred_s, zred_r, zag_s, zag_r, ag_s, ag_r, out_sem,
):
    w, n = lax.axis_index("wide"), lax.axis_index("narrow")
    block = index_ref.shape[0]
    batch = block * narrow
    features, owned = cen.shape[2], cen.shape[1]
    stages = plan(wide, block)
    nst = len(stages)
    core = w % 2
    partner = (w + 1 - 2 * core, n)
    up = [2**k for k in range(1, nst)]
    masks = [1] + [jnp.where(core == 0, p, q) for p, q in zip(up, up[::-1])]
    side = [core] + [(w // m) % 2 for m in masks[1:]]
    peer = [partner] + [(w + m * (1 - 2 * s), n) for m, s in zip(masks[1:], side[1:])]
    start = [0]
    for s, (held, halves) in zip(side, stages):
        start.append(start[-1] + (s * held if halves else 0))
    start = [0] + [pl.multiple_of(s, SUB) for s in start[1:]]
    half = stages[0][0]

    loads = [
        pltpu.make_async_copy(src, dst, load_sem.at[i])
        for i, (src, dst) in enumerate(((tf_hbm, tf), (cen_hbm, cen.at[0]), (wgt_hbm, wgt.at[0]), (lab_hbm, lab)))
    ]
    for load in loads:
        load.start()
    zpeers = [(w, lax.rem(n + k, narrow)) for k in range(1, narrow)]
    barrier = pltpu.get_barrier_semaphore()
    for p in zpeers + peer:
        pl.semaphore_signal(barrier, inc=1, device_id=p, device_id_type=MESH)

    def copy(src, dst, ssem, rsem, to):
        return pltpu.make_async_remote_copy(
            src_ref=src, dst_ref=dst, send_sem=ssem, recv_sem=rsem, device_id=to, device_id_type=MESH
        )

    sent = []

    def send(*args, later=True):
        c = copy(*args)
        c.start()
        if later:
            sent.append(c)
        return c

    loads[0].wait()
    for g in range(block // SUB):
        picked = [tf[pl.ds(index_ref[g * SUB + i], 1), :] for i in range(SUB)]
        rows[n, pl.ds(g * SUB, SUB), :] = jnp.concatenate(picked, axis=0)
    pl.semaphore_wait(barrier, len(zpeers) + nst)

    def at(k):
        return lax.rem(n + k, narrow)

    def piece_of(j):
        held = stages[j][0]
        theirs = pl.multiple_of(start[j] + (1 - side[j]) * held, SUB)
        return pl.ds(start[j + 1], held), pl.ds(theirs, held)

    def spread(ref, zsem, sem, back, i, k):
        m = at(k)
        if i == 0:
            if k > 0:
                held = piece_of(back[0])[0]
                copy(ref.at[m, held], ref.at[m, held], zsem[0].at[k], zsem[1].at[k], partner).wait_recv()
        else:
            j = back[i - 1]
            theirs = piece_of(j)[1]
            copy(ref.at[m, theirs], ref.at[m, theirs], sem[0].at[j, k], sem[1].at[j, k], peer[j]).wait_recv()
        if i < len(back) and not (i == len(back) - 1 and back[i] == 0 and ref is rows):
            j = back[i]
            held = piece_of(j)[0]
            send(ref.at[m, held], ref.at[m, held], sem[0].at[j, k], sem[1].at[j, k], peer[j])

    def along_narrow(ref, held, zsem):
        for k in range(1, narrow):
            to = (w, lax.rem(n + narrow - k, narrow))
            send(ref.at[n, held], ref.at[n, held], zsem[0].at[k], zsem[1].at[k], to)

    cuts = [j for j in range(nst) if stages[j][1]][::-1]
    row_cuts = [j for j in cuts if j < ROW_DEPTH]
    mine, other = piece_of(0)
    along_narrow(rows, piece_of(row_cuts[0])[0], (zrow_s, zrow_r))

    loads[1].wait()
    send(cen.at[0], cen.at[1], pair_s.at[0], pair_r.at[0], partner)
    loads[2].wait()
    send(wgt.at[0], wgt.at[1], pair_s.at[1], pair_r.at[1], partner)
    ones = jnp.ones((SUB, features), jnp.float32)

    def squares(o):
        centers = cen[o]
        for i, term in enumerate(split(centers, 3)):
            cen_terms[o, i] = term
        return dot(ones, centers * centers, ((1,), (1,)))[0:1, :]

    center_sq = [squares(0)]

    def reduce_copy(j, k):
        m = at(k)
        held, halves = stages[j]
        first = start[j] + (1 - side[j]) * held if halves else start[j + 1]
        first = pl.multiple_of(first - core * half, SUB)
        return (
            part.at[m, pl.ds(first, held)], got[j - 1].at[k], red_s.at[j, k], red_r.at[j, k], peer[j]
        )

    sends = {}

    def begin(ks):
        piece = jnp.concatenate([rows[at(k), mine, :] for k in ks], axis=0)
        piece_sq = jnp.sum(piece * piece, axis=1, keepdims=True)
        piece_terms = split(piece, 3)
        total = 0.0
        for o in range(2):
            if len(center_sq) == o:
                copy(cen.at[0], cen.at[1], pair_s.at[0], pair_r.at[0], partner).wait_recv()
                center_sq.append(squares(o))
            inner = split_dot(piece_terms, [cen_terms[o, i] for i in range(3)])
            value = jnp.exp((2.0 * features - piece_sq - center_sq[o] + 2.0 * inner) / 128.0)
            for i, k in enumerate(ks):
                this = value[i * half : (i + 1) * half, :]
                if o == 0:
                    kern[at(k), mine, :] = this
                else:
                    away[k] = this
            if o == 1 and 0 in ks:
                copy(wgt.at[0], wgt.at[1], pair_s.at[1], pair_r.at[1], partner).wait_recv()
            if 0 in ks:
                for i, term in enumerate(split(wgt[o], 2)):
                    wgt_terms[o, i] = term
            total = total + split_dot(split(value, 2), [wgt_terms[o, i] for i in range(2)])
        for i, k in enumerate(ks):
            part[at(k)] = total[i * half : (i + 1) * half, :]
        for k in ks:
            sends[1, k] = send(*reduce_copy(1, k), later=stages[1][1])
        for k in ks:
            send(away.at[k], kern.at[at(k), mine], kern_s.at[k], kern_r.at[k], partner)

    def reduce(j, k):
        m = at(k)
        held, halves = stages[j]
        copy(*reduce_copy(j, k)).wait_recv()
        if not halves:
            sends[j, k].wait_send()
        keep = pl.ds(pl.multiple_of(start[j + 1] - core * half, SUB), held)
        part[m, keep, :] = part[m, keep, :] + got[j - 1][k]
        if j + 1 < nst:
            sends[j + 1, k] = send(*reduce_copy(j + 1, k), later=stages[j + 1][1])
        elif k > 0:
            send(part.at[m, keep], zgot.at[k], zred_s.at[k], zred_r.at[k], (w, m))

    begin([0])
    for i in range(len(row_cuts)):
        for k in range(1, narrow):
            spread(rows, (zrow_s, zrow_r), (row_s, row_r), row_cuts, i, k)
        if i + 1 < nst:
            reduce(i + 1, 0)
    for i in range(len(row_cuts) + 1, nst):
        reduce(i, 0)
    begin(list(range(1, narrow)))
    for j in range(1, nst):
        for k in range(1, narrow):
            reduce(j, k)

    last = stages[-1][0]
    keep = pl.ds(start[nst], last)
    loads[3].wait()
    column = lax.broadcasted_iota(jnp.int32, (1, lab.shape[1]), 1)
    chosen = [jnp.where(column == index_ref[start[nst] + i], 1.0, 0.0) for i in range(last)]
    tgt[...] = dot(jnp.concatenate(chosen, axis=0), lab[...], ((1,), (1,)))
    own = pl.ds(pl.multiple_of(start[nst] - core * half, SUB), last)
    total = part[n, own, :]
    for k in range(1, narrow):
        copy(part.at[n, own], zgot.at[k], zred_s.at[k], zred_r.at[k], partner).wait_recv()
        total = total + zgot[k]
    resid[n, keep, :] = total * (1.0 / math.sqrt(count)) - tgt[...]

    along_narrow(resid, keep, (zag_s, zag_r))
    for k in range(narrow):
        copy(away.at[k], kern.at[at(k), other], kern_s.at[k], kern_r.at[k], partner).wait_recv()
    outs = [pltpu.make_async_copy(kern, kern_hbm, out_sem.at[0])]
    outs[0].start()
    tail = len(cuts)
    order = [(0, 0), (1, 0)] if tail else [(0, 0)]
    for i in range(tail + 1):
        order += [(i, k) for k in range(1, narrow)]
        order += [(i + 2, 0)] if i + 2 <= tail else []
    for i, k in order:
        spread(resid, (zag_s, zag_r), (ag_s, ag_r), cuts, i, k)
        if i == tail:
            m = at(k)
            outs.append(pltpu.make_async_copy(resid.at[m], all_hbm.at[m], out_sem.at[1 + k]))
            outs[-1].start()
            if k == 0:
                outs.append(pltpu.make_async_copy(resid.at[n], res_hbm, out_sem.at[1 + narrow]))
                outs[-1].start()
    for c in sent:
        c.wait_send()
    for c in outs:
        c.wait()


def per_device(batch_index, train_features, train_labels, centers, weights):
    wide, narrow = lax.axis_size("wide"), lax.axis_size("narrow")
    block, features = batch_index.shape[0], centers.shape[1]
    outputs, owned = weights.shape[1], centers.shape[0]
    labels_t, weights_t = train_labels.T, weights.T
    stages = plan(wide, block)
    nst, last = len(stages), stages[-1][0]
    f32, dma = jnp.float32, pltpu.SemaphoreType.DMA
    anywhere = pl.BlockSpec(memory_space=pl.ANY)
    kernel, every, residual = pl.pallas_call(
        functools.partial(step_kernel, wide, narrow, owned * wide * narrow),
        out_shape=(
            jax.ShapeDtypeStruct((narrow, block, owned), f32),
            jax.ShapeDtypeStruct((narrow, block, outputs), f32),
            jax.ShapeDtypeStruct((block, outputs), f32),
        ),
        in_specs=[pl.BlockSpec(memory_space=pltpu.SMEM)] + [anywhere] * 4,
        out_specs=(anywhere, anywhere, anywhere),
        scratch_shapes=[
            pltpu.VMEM(train_features.shape, f32),
            pltpu.VMEM(labels_t.shape, f32),
            pltpu.VMEM((2, *centers.shape), f32),
            pltpu.VMEM((2, *weights_t.shape), f32),
            pltpu.VMEM((2, 3, *centers.shape), jnp.bfloat16),
            pltpu.VMEM((2, 2, *weights_t.shape), jnp.bfloat16),
            pltpu.VMEM((narrow, block, features), f32),
            pltpu.VMEM((narrow, block, owned), f32),
            pltpu.VMEM((narrow, block // 2, owned), f32),
            pltpu.VMEM((narrow, block // 2, outputs), f32),
            pltpu.VMEM((narrow, block, outputs), f32),
            pltpu.VMEM((last, outputs), f32),
            [pltpu.VMEM((narrow, held, outputs), f32) for held, _ in stages[1:]],
            pltpu.VMEM((narrow, last, outputs), f32),
            dma((4,)),
            dma((narrow,)), dma((narrow,)),
            dma((nst, narrow)), dma((nst, narrow)),
            dma((2,)), dma((2,)),
            dma((narrow,)), dma((narrow,)),
            dma((nst, narrow)), dma((nst, narrow)),
            dma((narrow,)), dma((narrow,)),
            dma((narrow,)), dma((narrow,)),
            dma((nst, narrow)), dma((nst, narrow)),
            dma((2 + narrow,)),
        ],
        compiler_params=pltpu.CompilerParams(
            collective_id=0, has_side_effects=True, vmem_limit_bytes=60 * 2**20
        ),
    )(batch_index, train_features, labels_t, centers, weights_t)
    batch = narrow * block
    delta = lax.dot_general(
        kernel.reshape(batch, owned), every.reshape(batch, outputs), (((0,), (0,)), ((), ())),
        precision=lax.Precision.HIGH, preferred_element_type=f32,
    )
    return weights - step_size / batch * delta, residual


def solution(mesh):
    in_specs = (
        P("narrow"),
        P("narrow", None),
        P("narrow", None),
        P(("wide", "narrow"), None),
        P(("wide", "narrow"), None),
    )
    out_specs = (P(("wide", "narrow"), None), P("narrow", None))
    return jax.shard_map(
        per_device, mesh=mesh, in_specs=in_specs, out_specs=out_specs, check_vma=False
    )
```
